512 devices in a mesh: out: 16 (over x, y_hi, core), in: 32 (over z, y_lo).
Axes of the slice: x: 4, y: 4 (y_hi: 2, y_lo: 2; y = y_hi * 2 + y_lo), z: 16, core: 2. Of those that a mesh axis runs over, the one named last changes fastest.
Arguments:
- kernel_weights: bfloat16 [2, 16384, 32768], P(None, 'out', 'in'), may hold values from -0.03125 to 0.03125
- mode_field: bfloat16 [32768, 1024], P('in', 'out'), may hold values from -6 to 6
- diff_blocks: bfloat16 [2, 16384, 1024], P(None, 'out', 'in'), may hold values from -6 to 6
- block_table: int32 [16, 32], replicated, may hold values from 0 to 15, as said below
Outputs:
- gain: bfloat16 [16384, 1024], P('out', 'in')
The draws below stay inside these ranges and needn't reach their ends.
Inputs may be any that keep to these rules, and one draw needn't show every extreme that they name: `block_table`: in every column the entries are 0 to 15, each once.
All inputs are finite; a program needn't handle non-finite values.
Results may differ from the reference program's by a relative error of at most 0.001.
Values may be sent and summed in bfloat16 or wider, within the bound.
A program may use at most 64 MiB of HBM per device.

```python
import jax
import jax.numpy as jnp
from jax import lax

TO = 1024
TI = 1024
TERMS = 2
CELLS = 1024
K_OUT = 16384
L_IN = 32768
NBLK = 16
NCOL = 32


def draw_block_table(key, part):
    column_keys = jax.random.split(jax.random.fold_in(key, 7), NCOL)
    columns = jax.vmap(lambda column_key: jax.random.permutation(column_key, NBLK))(column_keys)
    return columns.T.astype(jnp.int32)


def block_scale(key, dims, shards, smallest, high):
    def one(axis_at, shards_of):
        draws = jax.random.uniform(jax.random.fold_in(jax.random.fold_in(key, 6), axis_at), (shards_of,), jnp.float32, smallest / len(shards), high / len(shards))
        return jnp.repeat(jnp.exp(draws), dims[axis_at] // shards_of).reshape((-1,) + (1,) * (len(dims) - axis_at - 1))

    gain = one(*shards[0])
    for cut in shards[1:]:
        gain = gain * one(*cut)
    return gain


def centred(own_key, extent, scale, most, shards=(), kind=jnp.bfloat16):
    values = jax.random.normal(own_key, extent, jnp.float32) * scale
    if len(shards) > 0:
        values = block_scale(own_key, extent, shards, -0.22, 0.18) * values
    return jnp.clip(values, min=-most, max=most).astype(kind)


def setup_inputs(seed: int = 0) -> dict:
    key_of = jax.random.split(jax.random.key(seed), 5)
    kernel_weights = centred(key_of[0], (TERMS, K_OUT, L_IN), L_IN ** -0.5, 0.03125, ((1, 16), (2, 32)))
    mode_field = centred(key_of[1], (L_IN, CELLS), 1.0, 6.0, ((0, 32), (1, 16)))
    diff_blocks = centred(key_of[2], (TERMS, NBLK * TO, CELLS), 1.0, 6.0, ((1, 16), (2, 32)))
    block_table = draw_block_table(jax.random.fold_in(key_of[4], 71), 0)
    return dict(kernel_weights=kernel_weights, mode_field=mode_field, diff_blocks=diff_blocks, block_table=block_table)


def reference(kernel_weights, mode_field, diff_blocks, block_table):
    def one_row(row_index):
        def accumulate(running, col_index):
            tile = lax.dynamic_slice(kernel_weights, (jnp.int32(0), (row_index * TO).astype(jnp.int32), (col_index * TI).astype(jnp.int32)), (TERMS, TO, TI))
            inputs = lax.dynamic_slice_in_dim(mode_field, (col_index * TI).astype(jnp.int32), TI, 0)
            wanted = block_table[row_index, col_index]
            chosen = lax.dynamic_slice_in_dim(diff_blocks, (wanted * TO).astype(jnp.int32), TO, 1)
            for term_index in range(TERMS):
                product = jnp.dot(tile[term_index], inputs, preferred_element_type=jnp.float32)
                running = running + chosen[term_index].astype(jnp.float32) * product
            return running, None
        total, _ = lax.scan(accumulate, jnp.zeros((TO, CELLS), jnp.float32), jnp.arange(NCOL, dtype=jnp.int32))
        return total.astype(jnp.bfloat16)
    rows_all = lax.map(one_row, jnp.arange(NBLK, dtype=jnp.int32))
    return rows_all.reshape(K_OUT, CELLS)
```

```python
import jax
import jax.numpy as jnp
from jax import lax
from jax.sharding import Mesh, PartitionSpec as P

PLANE = ("out", "ylo")


def shards(kernel_weights, mode_field, diff_blocks, block_table):
    terms, rows, depth = kernel_weights.shape
    own_cells = diff_blocks.shape[2]
    out_n = lax.axis_size("out")
    ylo_n = lax.axis_size("ylo")
    z_n = lax.axis_size("z")
    z_index = lax.axis_index("z")
    piece = rows // (out_n * ylo_n)
    cells = own_cells * ylo_n * z_n

    weights = lax.all_to_all(kernel_weights, PLANE, split_axis=1, concat_axis=1, tiled=True)
    weights = weights.reshape(terms, out_n, ylo_n, piece, depth)
    field = lax.all_gather(mode_field.T, PLANE, axis=0, tiled=True)
    field = field.reshape(out_n, ylo_n, cells // out_n, depth)
    blocks = lax.all_to_all(diff_blocks, PLANE, split_axis=1, concat_axis=1, tiled=True)
    blocks = lax.all_gather(blocks, "z", axis=0)
    blocks = blocks.reshape(z_n, terms, out_n, ylo_n, piece, own_cells)
    blocks = blocks.transpose(2, 1, 4, 0, 3, 5).reshape(out_n, terms, piece, cells)

    total = jnp.zeros((out_n, piece, cells), jnp.float32)
    for y in range(ylo_n):
        column = lax.dynamic_index_in_dim(block_table, z_index * ylo_n + y, 1, keepdims=False)
        chosen = jnp.take(blocks, column, axis=0, mode="clip")
        here = field[:, y].reshape(cells, depth)
        for t in range(terms):
            product = lax.dot_general(
                weights[t, :, y].reshape(out_n * piece, depth), here,
                (((1,), (1,)), ((), ())), preferred_element_type=jnp.float32)
            total = total + chosen[:, t].astype(jnp.float32) * product.reshape(out_n, piece, cells)
    summed = lax.psum_scatter(total, "z", scatter_dimension=2, tiled=True)
    summed = summed.astype(jnp.bfloat16).reshape(out_n, piece, ylo_n, own_cells)
    summed = summed.transpose(0, 2, 1, 3).reshape(out_n * ylo_n * piece, own_cells)
    return lax.all_to_all(summed, PLANE, split_axis=0, concat_axis=0, tiled=True)


def solution(mesh):
    out_n, in_n = mesh.devices.shape
    fine = Mesh(mesh.devices.reshape(out_n, in_n // 2, 2), ("out", "z", "ylo"))
    both = ("z", "ylo")
    in_specs = (P(None, "out", both), P(both, "out"), P(None, "out", both), P())
    return jax.shard_map(shards, mesh=fine, in_specs=in_specs, out_specs=P("out", both), check_vma=False)
```

```python
import jax
import jax.numpy as jnp
from jax import lax
from jax.experimental import pallas as pl
from jax.experimental.pallas import tpu as pltpu
from jax.sharding import PartitionSpec as P

MESH = pl.DeviceIdType.MESH
BF16, F32, I32 = jnp.bfloat16, jnp.float32, jnp.int32

NP, NZ, NR = 4, 16, 16
TERMS, ROWS, DEPTH, CELLS = 2, 1024, 1024, 1024
PIECE, HALF = 32, 16
OWN = 32
FIELD = 64
CHUNK = 64
LANES = NR * HALF

OFFSETS = (1, 3, 2)
FAR = ((2, 2), (2, 1), (1, 2), (2, 3), (3, 2), (2, 0), (0, 2), (1, 1), (3, 3), (1, 3), (3, 1), (1, 0), (0, 1), (3, 0), (0, 3))
PEERS = tuple((dx, dy, dc) for dc in (0, 1) for dx, dy in FAR) + ((0, 0, 1),)
EARLY = 10


def rem(a, n):
    return lax.rem(a, jnp.int32(n))


def hot(shape, rule):
    rows = lax.broadcasted_iota(I32, shape, 0)
    lanes = lax.broadcasted_iota(I32, shape, 1)
    return jnp.where(rule(rows, lanes), 1.0, 0.0).astype(BF16)


def dot(a, b):
    return jnp.dot(a, b, preferred_element_type=F32)


def dot_nt(a, b):
    return lax.dot_general(a, b, (((1,), (1,)), ((), ())), preferred_element_type=F32)


def kernel(table, w_hbm, m_hbm, d_ref, out_ref,
           weights, field, packed, packets, blocks, spread, pick, unpack, results, finals, give_r, give_l, take_r, take_l, sums,
           own_sem, d_send, d_recv, m_send, m_recv, w_send, w_recv, b_send, b_recv, r_send, r_recv, l_send, l_recv, f_send, f_recv):
    o, i = lax.axis_index("out"), lax.axis_index("in")
    x, y_hi, core = o // 4, rem(o // 2, 2), rem(o, 2)
    z, y_lo = i // 2, rem(i, 2)
    y = y_hi * 2 + y_lo
    me = o * 2 + y_lo

    def place(dx, dy, dc=0, dz=0):
        px, py, pc, pz = rem(x + dx, NP), rem(y + dy, NP), rem(core + dc, 2), rem(z + dz, NZ)
        return px * 4 + (py // 2) * 2 + pc, pz * 2 + rem(py, 2)

    def piece_of(device):
        return device[0] * 2 + rem(device[1], 2)

    def remote(src, dst, send, recv, device):
        return pltpu.make_async_remote_copy(src, dst, send, recv, device_id=device, device_id_type=MESH)

    up, down = place(0, 0, 0, 1), place(0, 0, 0, NZ - 1)
    devices = [place(*p) for p in PEERS]
    sources = [place(NP - p[0], NP - p[1], p[2]) for p in PEERS]
    sends = []

    def packing(rows, lanes):
        return (rows // 128 == rem(lanes, 128) // 32) & (rem(rows, 128) == (lanes // 128) * 32 + rem(lanes, 32))

    wide = hot((512, 512), packing)
    flat = d_ref[...].reshape(TERMS * OWN, ROWS)
    stacked = jnp.concatenate(
        [jnp.concatenate([flat[b * 16:(b + 1) * 16, t * 128:(t + 1) * 128] for b in range(4)], axis=1) for t in range(8)], axis=0)
    packed[...] = dot(stacked, wide).astype(BF16).reshape(8, 16, 512)

    barrier = pltpu.get_barrier_semaphore()
    for device in devices + [up, down]:
        pl.semaphore_signal(barrier, inc=1, device_id=device, device_id_type=MESH)
    pl.semaphore_wait(barrier, len(devices) + 2)

    def packet(piece):
        return packed.at[piece // 4, :, pl.ds(pl.multiple_of(rem(piece, 4) * 128, 128), 128)]

    def packet_slot(device):
        return packets.at[rem(device[1], 2), :, pl.ds(pl.multiple_of(device[0] * 128, 128), 128)]

    def run(copy):
        copy.start()
        sends.append(copy)

    for n, device in enumerate(devices):
        run(remote(packet(piece_of(device)), packet_slot((o, i)), d_send.at[n], d_recv.at[n], device))
    own_packet = pltpu.make_async_copy(packet(me), packet_slot((o, i)), own_sem.at[0])
    own_packet.start()

    def along(a, b):
        return a * (1 - core) + b * core, b * (1 - core) + a * core

    def shard(dx, dy, dc=0):
        device = place(dx, dy, dc)
        return field.at[rem(device[1], 2), pl.ds(pl.multiple_of(device[0] * FIELD, FIELD), FIELD), :]

    partner = place(0, 0, 1)
    own_field = pltpu.make_async_copy(m_hbm, shard(0, 0), own_sem.at[1])
    own_field.start()
    for n, a in enumerate(OFFSETS):
        run(remote(m_hbm, shard(0, 0), m_send.at[n], m_recv.at[n], place(*along(a, 0))))
    for n, a in enumerate(OFFSETS):
        run(remote(m_hbm, shard(0, 0), m_send.at[3 + n], m_recv.at[3 + n], place(*along(0, a))))
    run(remote(m_hbm, shard(0, 0), m_send.at[15], m_recv.at[15], partner))

    def slab(half, device):
        return weights.at[half, rem(device[1], 2), :, pl.ds(pl.multiple_of(device[0] * HALF, HALF), HALF), :]

    def rows_for(half, piece):
        return w_hbm.at[:, pl.ds(pl.multiple_of(piece * PIECE + half * HALF, HALF), HALF), :]

    def send_weights(half, first, last):
        for n in range(first, last):
            run(remote(rows_for(half, piece_of(devices[n])), slab(half, (o, i)), w_send.at[half, n], w_recv.at[half, n], devices[n]))

    own_weights = [pltpu.make_async_copy(rows_for(half, me), slab(half, (o, i)), own_sem.at[2 + half]) for half in range(2)]
    for copy in own_weights:
        copy.start()
    send_weights(0, 0, EARLY)

    def unpacking(rows, lanes):
        return (rem(lanes, 128) // 16 == rows // 128) & (rem(rows, 128) == (lanes // 128) * 16 + rem(lanes, 16))

    spread[...] = hot((1024, 1024), unpacking)

    own_packet.wait()
    for n, source in enumerate(sources):
        remote(packet(me), packet_slot(source), d_send.at[n], d_recv.at[n], source).wait_recv()
    for q in range(2):
        opened = dot(packets[...].reshape(32, 2048)[:, q * 1024:(q + 1) * 1024], spread[...]).astype(BF16)
        for b in range(4):
            for half in range(2):
                for s in range(2):
                    row = (b // 2) * 64 + s * 32 + (b % 2) * 16
                    lane = (b * 2 + half) * 128
                    blocks[z, half, row:row + 16, q * 128:(q + 1) * 128] = opened[s * 16:(s + 1) * 16, lane:lane + 128]

    def ring_send(k):
        for half in range(2):
            if k < 8:
                at = blocks.at[rem(z - k + NZ, NZ), half]
                run(remote(at, at, b_send.at[0, half, k], b_recv.at[0, half, k], up))
            if k < 7:
                at = blocks.at[rem(z + k, NZ), half]
                run(remote(at, at, b_send.at[1, half, k], b_recv.at[1, half, k], down))

    def ring_wait(k):
        for half in range(2):
            if k < 8:
                at = blocks.at[rem(z - k - 1 + NZ, NZ), half]
                remote(at, at, b_send.at[0, half, k], b_recv.at[0, half, k], down).wait_recv()
            if k < 7:
                at = blocks.at[rem(z + k + 1, NZ), half]
                remote(at, at, b_send.at[1, half, k], b_recv.at[1, half, k], up).wait_recv()

    ring_send(0)

    own_field.wait()
    for m, a in enumerate(OFFSETS):
        here = shard(*along(NP - a, 0))
        remote(here, here, m_send.at[m], m_recv.at[m], place(*along(a, 0))).wait_recv()
        for n, b in enumerate(OFFSETS):
            slot = 6 + m * 3 + n
            run(remote(here, here, m_send.at[slot], m_recv.at[slot], place(*along(0, b))))
        run(remote(here, here, m_send.at[16 + m], m_recv.at[16 + m], partner))

    send_weights(0, EARLY, len(PEERS))
    send_weights(1, 0, len(PEERS))

    def forward_field(m, n):
        a = 0 if m == 0 else NP - OFFSETS[m - 1]
        slot = 3 + m * 3 + n
        here = shard(*along(a, NP - OFFSETS[n]))
        remote(here, here, m_send.at[slot], m_recv.at[slot], place(*along(0, OFFSETS[n]))).wait_recv()
        back = 19 + m * 3 + n
        run(remote(here, here, m_send.at[back], m_recv.at[back], partner))

    ring_wait(0)
    ring_send(1)
    for n in range(3):
        forward_field(0, n)
    ring_wait(1)
    ring_send(2)
    for m in range(1, 4):
        for n in range(3):
            forward_field(m, n)

    for s in range(2):
        lanes = lax.broadcasted_iota(I32, (1, LANES), 1)
        wanted = jnp.zeros((1, LANES), I32)
        for r in range(NR):
            wanted = jnp.where(lanes // HALF == r, table[r, z * 2 + s], wanted)
        pick[s] = hot((LANES, LANES), lambda rows, cols: (rows // HALF == wanted) & (rem(rows, HALF) == rem(cols, HALF)))

    def closing(rows, lanes):
        inner = rem(lanes, 128)
        return (inner // 16 == rows // 128) & (rem(rows, 128) == (lanes // 128) * 16 + rem(lanes, 16))

    spread[0:512, :] = hot((512, 1024), closing)
    for b in range(2):
        unpack[b] = hot((512, 128), lambda rows, lanes: (rows // 128 == lanes // 32) & (rem(rows, 128) == b * 32 + rem(lanes, 32)))

    for k in range(2, 7):
        ring_wait(k)
        ring_send(k + 1)
    ring_wait(7)

    for n in range(16):
        if n == 0:
            here = shard(0, 0, 1)
        elif n < 4:
            a = NP - OFFSETS[n - 1]
            here = shard(a * core, a * (1 - core), 1)
        else:
            m, q = (n - 4) // 3, (n - 4) % 3
            a = 0 if m == 0 else NP - OFFSETS[m - 1]
            b = NP - OFFSETS[q]
            here = shard(a * core + b * (1 - core), b * core + a * (1 - core), 1)
        remote(here, here, m_send.at[15 + n], m_recv.at[15 + n], partner).wait_recv()

    def chunk_pair(half, first, second):
        total = None
        for s in range(2):
            cells = jnp.concatenate(
                [field[s, pl.ds(pl.multiple_of(first * CHUNK, CHUNK), CHUNK), :],
                 field[s, pl.ds(pl.multiple_of(second * CHUNK, CHUNK), CHUNK), :]], axis=0)
            product = dot_nt(cells, weights[half, s].reshape(TERMS * LANES, DEPTH))
            chosen = dot(jnp.concatenate([blocks[first, half], blocks[second, half]], axis=0), pick[s])
            for t in range(TERMS):
                scale = jnp.concatenate([chosen[t * 64:t * 64 + 64], chosen[128 + t * 64:192 + t * 64]], axis=0)
                part = scale * product[:, t * LANES:(t + 1) * LANES]
                total = part if total is None else total + part
        return total

    def right(half, k, sub):
        return remote(give_r.at[half, k, sub], take_r.at[half, k, sub], r_send.at[half, k, sub], r_recv.at[half, k, sub], up)

    def left(half, k, sub):
        return remote(give_l.at[half, k, sub], take_l.at[half, k, sub], l_send.at[half, k, sub], l_recv.at[half, k, sub], down)

    for half in range(2):
        own_weights[half].wait()
        for n, source in enumerate(sources):
            remote(rows_for(half, me), slab(half, source), w_send.at[half, n], w_recv.at[half, n], source).wait_recv()

        total = chunk_pair(half, rem(z + 8, NZ), rem(z + 9, NZ))
        for sub in range(2):
            give_r[half, 0, sub] = total[:CHUNK, sub * 128:(sub + 1) * 128]
            right(half, 0, sub).start()
            give_l[half, 0, sub] = total[CHUNK:, sub * 128:(sub + 1) * 128]
            left(half, 0, sub).start()

        def ring_step(k, carry, half=half):
            total = chunk_pair(half, rem(z + 8 - k + NZ, NZ), rem(z + 9 + k, NZ))
            for sub in range(2):
                right(half, k - 1, sub).wait_recv()
                give_r[half, k, sub] = total[:CHUNK, sub * 128:(sub + 1) * 128] + take_r[half, k - 1, sub]
                right(half, k, sub).start()
                left(half, k - 1, sub).wait_recv()
                give_l[half, k, sub] = total[CHUNK:, sub * 128:(sub + 1) * 128] + take_l[half, k - 1, sub]

                @pl.when(k < 7)
                def _():
                    left(half, k, sub).start()
            return carry

        lax.fori_loop(1, 8, ring_step, jnp.int32(0))

    for half in range(2):
        for sub in range(2):
            right(half, 7, sub).wait_recv()
            sums[half * 2 + sub] = (give_l[half, 7, sub] + take_r[half, 7, sub]).astype(BF16)

    closed = jnp.concatenate(
        [jnp.concatenate([sums[half * 2 + q, s * 32 + b * 16:s * 32 + b * 16 + 16, :] for b in range(2) for half in range(2)], axis=1)
         for s in range(2) for q in range(2)], axis=0)
    results[...] = dot(closed, spread[0:512, :]).astype(BF16).reshape(2, 2, 16, 1024)

    def result_for(device):
        return results.at[rem(device[1], 2), device[0] // 8, :, pl.ds(pl.multiple_of(rem(device[0], 8) * 128, 128), 128)]

    def result_slot(piece):
        return finals.at[piece // 4, :, pl.ds(pl.multiple_of(rem(piece, 4) * 128, 128), 128)]

    for n, device in enumerate(devices):
        run(remote(result_for(device), result_slot(me), f_send.at[n], f_recv.at[n], device))
    own_result = pltpu.make_async_copy(result_for((o, i)), result_slot(me), own_sem.at[4])
    own_result.start()

    for copy in sends[:-len(devices)]:
        copy.wait_send()
    for half in range(2):
        for sub in range(2):
            for k in range(8):
                right(half, k, sub).wait_send()
                if k < 7:
                    left(half, k, sub).wait_send()

    own_result.wait()
    for n, source in enumerate(sources):
        remote(result_for(source), result_slot(piece_of(source)), f_send.at[n], f_recv.at[n], source).wait_recv()
    for b in range(2):
        opened = dot(finals[...].reshape(128, 512), unpack[b]).astype(BF16)
        for j in range(8):
            out_ref[b * 16:(b + 1) * 16, j * 128:(j + 1) * 128] = opened[j * 16:(j + 1) * 16, :]
    for copy in sends[-len(devices):]:
        copy.wait_send()


def shards(kernel_weights, mode_field, diff_blocks, block_table):
    peers = len(PEERS)
    dma = pltpu.SemaphoreType.DMA
    vmem = pl.BlockSpec(memory_space=pltpu.VMEM)
    gain = pl.pallas_call(
        kernel,
        out_shape=jax.ShapeDtypeStruct((OWN, ROWS), BF16),
        in_specs=[pl.BlockSpec(memory_space=pltpu.SMEM), pl.BlockSpec(memory_space=pl.ANY),
                  pl.BlockSpec(memory_space=pl.ANY), vmem],
        out_specs=vmem,
        scratch_shapes=[
            pltpu.VMEM((2, 2, TERMS, LANES, DEPTH), BF16),
            pltpu.VMEM((2, CELLS, DEPTH), BF16),
            pltpu.VMEM((8, 16, 512), BF16),
            pltpu.VMEM((2, 16, 2048), BF16),
            pltpu.VMEM((NZ, 2, TERMS * CHUNK, LANES), BF16),
            pltpu.VMEM((1024, 1024), BF16),
            pltpu.VMEM((2, LANES, LANES), BF16),
            pltpu.VMEM((2, 512, 128), BF16),
            pltpu.VMEM((2, 2, 16, 1024), BF16),
            pltpu.VMEM((8, 16, 512), BF16),
            pltpu.VMEM((2, 8, 2, CHUNK, 128), F32),
            pltpu.VMEM((2, 8, 2, CHUNK, 128), F32),
            pltpu.VMEM((2, 8, 2, CHUNK, 128), F32),
            pltpu.VMEM((2, 8, 2, CHUNK, 128), F32),
            pltpu.VMEM((4, CHUNK, 128), BF16),
            dma((5,)),
            dma((peers,)), dma((peers,)),
            dma((31,)), dma((31,)),
            dma((2, peers)), dma((2, peers)),
            dma((2, 2, 8)), dma((2, 2, 8)),
            dma((2, 8, 2)), dma((2, 8, 2)),
            dma((2, 8, 2)), dma((2, 8, 2)),
            dma((peers,)), dma((peers,)),
        ],
        compiler_params=pltpu.CompilerParams(collective_id=0, has_side_effects=True, vmem_limit_bytes=48 * 2**20),
        name="collision_gain",
    )(block_table, kernel_weights, mode_field.T, diff_blocks.transpose(0, 2, 1))
    return gain.T


def solution(mesh):
    in_specs = (P(None, "out", "in"), P("in", "out"), P(None, "out", "in"), P())
    return jax.shard_map(shards, mesh=mesh, in_specs=in_specs, out_specs=P("out", "in"), check_vma=False)
```

```python
import jax
import jax.numpy as jnp
from jax import lax
from jax.experimental import pallas as pl
from jax.experimental.pallas import tpu as pltpu
from jax.sharding import PartitionSpec as P

MESH = pl.DeviceIdType.MESH
BF16, F32, I32 = jnp.bfloat16, jnp.float32, jnp.int32

NP, NZ, NR = 4, 16, 16
TERMS, ROWS, DEPTH, CELLS = 2, 1024, 1024, 1024
PIECE, HALF = 32, 16
OWN = 32
FIELD = 64
CHUNK = 64
LANES = NR * HALF

OFFSETS = (1, 3, 2)
FAR = ((2, 2), (2, 1), (1, 2), (2, 3), (3, 2), (2, 0), (0, 2), (1, 1), (3, 3), (1, 3), (3, 1), (1, 0), (0, 1), (3, 0), (0, 3))
PEERS = tuple((dx, dy, dc) for dc in (0, 1) for dx, dy in FAR) + ((0, 0, 1),)
EARLY = 12


def rem(a, n):
    return lax.rem(a, jnp.int32(n))


def hot(shape, rule):
    rows = lax.broadcasted_iota(I32, shape, 0)
    lanes = lax.broadcasted_iota(I32, shape, 1)
    return jnp.where(rule(rows, lanes), 1.0, 0.0).astype(BF16)


def dot(a, b):
    return jnp.dot(a, b, preferred_element_type=F32)


def dot_nt(a, b):
    return lax.dot_general(a, b, (((1,), (1,)), ((), ())), preferred_element_type=F32)


def kernel(table, w_hbm, m_hbm, d_ref, out_ref,
           weights, field, packed, packets, blocks, spread, pick, unpack, results, finals, give_r, give_l, take_r, take_l, sums,
           own_sem, d_send, d_recv, m_send, m_recv, w_send, w_recv, b_send, b_recv, r_send, r_recv, l_send, l_recv, f_send, f_recv):
    o, i = lax.axis_index("out"), lax.axis_index("in")
    x, y_hi, core = o // 4, rem(o // 2, 2), rem(o, 2)
    z, y_lo = i // 2, rem(i, 2)
    y = y_hi * 2 + y_lo
    me = o * 2 + y_lo

    def place(dx, dy, dc=0, dz=0):
        px, py, pc, pz = rem(x + dx, NP), rem(y + dy, NP), rem(core + dc, 2), rem(z + dz, NZ)
        return px * 4 + (py // 2) * 2 + pc, pz * 2 + rem(py, 2)

    def piece_of(device):
        return device[0] * 2 + rem(device[1], 2)

    def remote(src, dst, send, recv, device):
        return pltpu.make_async_remote_copy(src, dst, send, recv, device_id=device, device_id_type=MESH)

    up, down = place(0, 0, 0, 1), place(0, 0, 0, NZ - 1)
    up_two, down_two = place(0, 0, 0, 2), place(0, 0, 0, NZ - 2)
    devices = [place(*p) for p in PEERS]
    sources = [place(NP - p[0], NP - p[1], p[2]) for p in PEERS]
    sends = []

    def packing(rows, lanes):
        return (rows // 128 == rem(lanes, 128) // 32) & (rem(rows, 128) == (lanes // 128) * 32 + rem(lanes, 32))

    wide = hot((512, 512), packing)
    flat = d_ref[...].reshape(TERMS * OWN, ROWS)
    stacked = jnp.concatenate(
        [jnp.concatenate([flat[b * 16:(b + 1) * 16, t * 128:(t + 1) * 128] for b in range(4)], axis=1) for t in range(8)], axis=0)
    packed[...] = dot(stacked, wide).astype(BF16).reshape(8, 16, 512)

    barrier = pltpu.get_barrier_semaphore()
    for device in devices + [up, down, up_two, down_two]:
        pl.semaphore_signal(barrier, inc=1, device_id=device, device_id_type=MESH)
    pl.semaphore_wait(barrier, len(devices) + 4)

    def packet(piece):
        return packed.at[piece // 4, :, pl.ds(pl.multiple_of(rem(piece, 4) * 128, 128), 128)]

    def packet_slot(device):
        return packets.at[rem(device[1], 2), :, pl.ds(pl.multiple_of(device[0] * 128, 128), 128)]

    def run(copy):
        copy.start()
        sends.append(copy)

    for n, device in enumerate(devices):
        run(remote(packet(piece_of(device)), packet_slot((o, i)), d_send.at[n], d_recv.at[n], device))
    own_packet = pltpu.make_async_copy(packet(me), packet_slot((o, i)), own_sem.at[0])
    own_packet.start()

    def along(a, b):
        return a * (1 - core) + b * core, b * (1 - core) + a * core

    def shard(dx, dy, dc=0):
        device = place(dx, dy, dc)
        return field.at[rem(device[1], 2), pl.ds(pl.multiple_of(device[0] * FIELD, FIELD), FIELD), :]

    partner = place(0, 0, 1)
    own_field = pltpu.make_async_copy(m_hbm, shard(0, 0), own_sem.at[1])
    own_field.start()
    for n, a in enumerate(OFFSETS):
        run(remote(m_hbm, shard(0, 0), m_send.at[n], m_recv.at[n], place(*along(a, 0))))
    for n, a in enumerate(OFFSETS):
        run(remote(m_hbm, shard(0, 0), m_send.at[3 + n], m_recv.at[3 + n], place(*along(0, a))))
    run(remote(m_hbm, shard(0, 0), m_send.at[15], m_recv.at[15], partner))

    def slab(half, device):
        return weights.at[half, rem(device[1], 2), :, pl.ds(pl.multiple_of(device[0] * HALF, HALF), HALF), :]

    def rows_for(half, piece):
        return w_hbm.at[:, pl.ds(pl.multiple_of(piece * PIECE + half * HALF, HALF), HALF), :]

    def send_weights(half, first, last):
        for n in range(first, last):
            run(remote(rows_for(half, piece_of(devices[n])), slab(half, (o, i)), w_send.at[half, n], w_recv.at[half, n], devices[n]))

    for half in range(2):
        pltpu.make_async_copy(rows_for(half, me), slab(half, (o, i)), own_sem.at[2 + half]).start()
    send_weights(0, 0, EARLY)

    def unpacking(rows, lanes):
        return (rem(lanes, 128) // 16 == rows // 128) & (rem(rows, 128) == (lanes // 128) * 16 + rem(lanes, 16))

    spread[...] = hot((1024, 1024), unpacking)

    own_packet.wait()
    for n, source in enumerate(sources):
        remote(packet(me), packet_slot(source), d_send.at[n], d_recv.at[n], source).wait_recv()
    for q in range(2):
        opened = dot(packets[...].reshape(32, 2048)[:, q * 1024:(q + 1) * 1024], spread[...]).astype(BF16)
        for b in range(4):
            for half in range(2):
                for s in range(2):
                    row = (b // 2) * 64 + s * 32 + (b % 2) * 16
                    lane = (b * 2 + half) * 128
                    blocks[z, half, row:row + 16, q * 128:(q + 1) * 128] = opened[s * 16:(s + 1) * 16, lane:lane + 128]

    def ring_send(k):
        for sub in range(4):
            lot = pl.ds(sub % 2 * 64, 64)
            if k < 8:
                at = blocks.at[rem(z - k + NZ, NZ), sub // 2, lot]
                run(remote(at, at, b_send.at[0, sub, k], b_recv.at[0, sub, k], up))
            if k < 7:
                at = blocks.at[rem(z + k, NZ), sub // 2, lot]
                run(remote(at, at, b_send.at[1, sub, k], b_recv.at[1, sub, k], down))

    def ring_pass(k):
        for sub in range(4):
            lot = pl.ds(sub % 2 * 64, 64)
            at = blocks.at[rem(z - k - 1 + NZ, NZ), sub // 2, lot]
            remote(at, at, b_send.at[0, sub, k], b_recv.at[0, sub, k], down).wait_recv()
            if k < 7:
                run(remote(at, at, b_send.at[0, sub, k + 1], b_recv.at[0, sub, k + 1], up))
                at = blocks.at[rem(z + k + 1, NZ), sub // 2, lot]
                remote(at, at, b_send.at[1, sub, k], b_recv.at[1, sub, k], up).wait_recv()
                if k < 6:
                    run(remote(at, at, b_send.at[1, sub, k + 1], b_recv.at[1, sub, k + 1], down))

    ring_send(0)

    own_field.wait()
    for m, a in enumerate(OFFSETS):
        here = shard(*along(NP - a, 0))
        remote(here, here, m_send.at[m], m_recv.at[m], place(*along(a, 0))).wait_recv()
        for n, b in enumerate(OFFSETS):
            slot = 6 + m * 3 + n
            run(remote(here, here, m_send.at[slot], m_recv.at[slot], place(*along(0, b))))
        run(remote(here, here, m_send.at[16 + m], m_recv.at[16 + m], partner))

    send_weights(0, EARLY, len(PEERS))
    send_weights(1, 0, len(PEERS))

    def forward_field(m, n):
        a = 0 if m == 0 else NP - OFFSETS[m - 1]
        slot = 3 + m * 3 + n
        here = shard(*along(a, NP - OFFSETS[n]))
        remote(here, here, m_send.at[slot], m_recv.at[slot], place(*along(0, OFFSETS[n]))).wait_recv()
        back = 19 + m * 3 + n
        run(remote(here, here, m_send.at[back], m_recv.at[back], partner))

    ring_pass(0)
    ring_pass(1)

    for s in range(2):
        lanes = lax.broadcasted_iota(I32, (1, LANES), 1)
        wanted = jnp.zeros((1, LANES), I32)
        for r in range(NR):
            wanted = jnp.where(lanes // HALF == r, table[r, z * 2 + s], wanted)
        pick[s] = hot((LANES, LANES), lambda rows, cols: (rows // HALF == wanted) & (rem(rows, HALF) == rem(cols, HALF)))

    def closing(rows, lanes):
        inner = rem(lanes, 128)
        return (inner // 16 == rows // 128) & (rem(rows, 128) == (lanes // 128) * 16 + rem(lanes, 16))

    spread[0:512, :] = hot((512, 1024), closing)
    for b in range(2):
        unpack[b] = hot((512, 128), lambda rows, lanes: (rows // 128 == lanes // 32) & (rem(rows, 128) == b * 32 + rem(lanes, 32)))

    ring_pass(2)
    ring_pass(3)
    for n in range(3):
        forward_field(0, n)
    ring_pass(4)
    for m in range(1, 4):
        for n in range(3):
            forward_field(m, n)
    for k in range(5, 8):
        ring_pass(k)

    for n in range(16):
        if n == 0:
            here = shard(0, 0, 1)
        elif n < 4:
            a = NP - OFFSETS[n - 1]
            here = shard(a * core, a * (1 - core), 1)
        else:
            m, q = (n - 4) // 3, (n - 4) % 3
            a = 0 if m == 0 else NP - OFFSETS[m - 1]
            b = NP - OFFSETS[q]
            here = shard(a * core + b * (1 - core), b * core + a * (1 - core), 1)
        remote(here, here, m_send.at[15 + n], m_recv.at[15 + n], partner).wait_recv()

    def chunk_pair(half, first, second):
        total = None
        for s in range(2):
            cells = jnp.concatenate(
                [field[s, pl.ds(pl.multiple_of(first * CHUNK, CHUNK), CHUNK), :],
                 field[s, pl.ds(pl.multiple_of(second * CHUNK, CHUNK), CHUNK), :]], axis=0)
            product = dot_nt(cells, weights[half, s].reshape(TERMS * LANES, DEPTH))
            chosen = dot(jnp.concatenate([blocks[first, half], blocks[second, half]], axis=0), pick[s])
            for t in range(TERMS):
                scale = jnp.concatenate([chosen[t * 64:t * 64 + 64], chosen[128 + t * 64:192 + t * 64]], axis=0)
                part = scale * product[:, t * LANES:(t + 1) * LANES]
                total = part if total is None else total + part
        return total

    def right(half, k, sub):
        target = up_two if k in (1, 3, 5) else up
        return remote(give_r.at[half, k, sub], take_r.at[half, k, sub], r_send.at[half, k, sub], r_recv.at[half, k, sub], target)

    def left(half, k, sub):
        target = down_two if k in (0, 2, 4) else down
        return remote(give_l.at[half, k, sub], take_l.at[half, k, sub], l_send.at[half, k, sub], l_recv.at[half, k, sub], target)

    def reduce_half(half, carry):
        pltpu.make_async_copy(rows_for(half, me), slab(half, (o, i)), own_sem.at[2 + half]).wait()
        for n, source in enumerate(sources):
            remote(rows_for(half, me), slab(half, source), w_send.at[half, n], w_recv.at[half, n], source).wait_recv()
        for k in range(8):
            total = chunk_pair(half, rem(z + 8 - k + NZ, NZ), rem(z + 9 + k, NZ))
            raw, chain = (right, left) if k % 2 == 0 else (left, right)
            give, take = (give_l, take_l) if k % 2 == 0 else (give_r, take_r)
            other = give_r if k % 2 == 0 else give_l
            raw_rows, chain_rows = (total[:CHUNK], total[CHUNK:]) if k % 2 == 0 else (total[CHUNK:], total[:CHUNK])
            for sub in range(2):
                other[half, k, sub] = raw_rows[:, sub * 128:(sub + 1) * 128]
                if k < 7:
                    raw(half, k, sub).start()
            for sub in range(2):
                value = chain_rows[:, sub * 128:(sub + 1) * 128]
                if k >= 1:
                    chain(half, k - 1, sub).wait_recv()
                    value = value + take[half, k - 1, sub]
                if k >= 2 and k - 2 >= k % 2:
                    chain(half, k - 2, sub).wait_recv()
                    value = value + take[half, k - 2, sub]
                give[half, k, sub] = value
                chain(half, k, sub).start()
        return carry

    lax.fori_loop(0, 2, reduce_half, jnp.int32(0))

    for half in range(2):
        for sub in range(2):
            left(half, 6, sub).wait_recv()
            right(half, 7, sub).wait_recv()
            total = give_l[half, 7, sub] + take_l[half, 6, sub] + take_r[half, 7, sub]
            sums[half * 2 + sub] = total.astype(BF16)

    closed = jnp.concatenate(
        [jnp.concatenate([sums[half * 2 + q, s * 32 + b * 16:s * 32 + b * 16 + 16, :] for b in range(2) for half in range(2)], axis=1)
         for s in range(2) for q in range(2)], axis=0)
    results[...] = dot(closed, spread[0:512, :]).astype(BF16).reshape(2, 2, 16, 1024)

    def result_for(device):
        return results.at[rem(device[1], 2), device[0] // 8, :, pl.ds(pl.multiple_of(rem(device[0], 8) * 128, 128), 128)]

    def result_slot(piece):
        return finals.at[piece // 4, :, pl.ds(pl.multiple_of(rem(piece, 4) * 128, 128), 128)]

    for n, device in enumerate(devices):
        run(remote(result_for(device), result_slot(me), f_send.at[n], f_recv.at[n], device))
    own_result = pltpu.make_async_copy(result_for((o, i)), result_slot(me), own_sem.at[4])
    own_result.start()

    for copy in sends[:-len(devices)]:
        copy.wait_send()
    for half in range(2):
        for sub in range(2):
            for k in range(8):
                right(half, k, sub).wait_send()
                if k < 7:
                    left(half, k, sub).wait_send()

    own_result.wait()
    for n, source in enumerate(sources):
        remote(result_for(source), result_slot(piece_of(source)), f_send.at[n], f_recv.at[n], source).wait_recv()
    for b in range(2):
        opened = dot(finals[...].reshape(128, 512), unpack[b]).astype(BF16)
        for j in range(8):
            out_ref[b * 16:(b + 1) * 16, j * 128:(j + 1) * 128] = opened[j * 16:(j + 1) * 16, :]
    for copy in sends[-len(devices):]:
        copy.wait_send()


def shards(kernel_weights, mode_field, diff_blocks, block_table):
    peers = len(PEERS)
    dma = pltpu.SemaphoreType.DMA
    vmem = pl.BlockSpec(memory_space=pltpu.VMEM)
    gain = pl.pallas_call(
        kernel,
        out_shape=jax.ShapeDtypeStruct((OWN, ROWS), BF16),
        in_specs=[pl.BlockSpec(memory_space=pltpu.SMEM), pl.BlockSpec(memory_space=pl.ANY),
                  pl.BlockSpec(memory_space=pl.ANY), vmem],
        out_specs=vmem,
        scratch_shapes=[
            pltpu.VMEM((2, 2, TERMS, LANES, DEPTH), BF16),
            pltpu.VMEM((2, CELLS, DEPTH), BF16),
            pltpu.VMEM((8, 16, 512), BF16),
            pltpu.VMEM((2, 16, 2048), BF16),
            pltpu.VMEM((NZ, 2, TERMS * CHUNK, LANES), BF16),
            pltpu.VMEM((1024, 1024), BF16),
            pltpu.VMEM((2, LANES, LANES), BF16),
            pltpu.VMEM((2, 512, 128), BF16),
            pltpu.VMEM((2, 2, 16, 1024), BF16),
            pltpu.VMEM((8, 16, 512), BF16),
            pltpu.VMEM((2, 8, 2, CHUNK, 128), F32),
            pltpu.VMEM((2, 8, 2, CHUNK, 128), F32),
            pltpu.VMEM((2, 8, 2, CHUNK, 128), F32),
            pltpu.VMEM((2, 8, 2, CHUNK, 128), F32),
            pltpu.VMEM((4, CHUNK, 128), BF16),
            dma((5,)),
            dma((peers,)), dma((peers,)),
            dma((31,)), dma((31,)),
            dma((2, peers)), dma((2, peers)),
            dma((2, 4, 8)), dma((2, 4, 8)),
            dma((2, 8, 2)), dma((2, 8, 2)),
            dma((2, 8, 2)), dma((2, 8, 2)),
            dma((peers,)), dma((peers,)),
        ],
        compiler_params=pltpu.CompilerParams(collective_id=0, has_side_effects=True, vmem_limit_bytes=63 * 2**20),
        name="collision_gain",
    )(block_table, kernel_weights, mode_field.T, diff_blocks.transpose(0, 2, 1))
    return gain.T


def solution(mesh):
    in_specs = (P(None, "out", "in"), P("in", "out"), P(None, "out", "in"), P())
    return jax.shard_map(shards, mesh=mesh, in_specs=in_specs, out_specs=P("out", "in"), check_vma=False)
```

```python
import jax
import jax.numpy as jnp
from jax import lax
from jax.experimental import pallas as pl
from jax.experimental.pallas import tpu as pltpu
from jax.sharding import PartitionSpec as P

MESH = pl.DeviceIdType.MESH
BF16, F32, I32 = jnp.bfloat16, jnp.float32, jnp.int32

NP, NZ, NR = 4, 16, 16
TERMS, ROWS, DEPTH, CELLS = 2, 1024, 1024, 1024
PIECE, HALF = 32, 16
OWN = 32
FIELD = 64
CHUNK = 64
LANES = NR * HALF

OFFSETS = (1, 3, 2)
FAR = ((2, 2), (2, 1), (1, 2), (2, 3), (3, 2), (2, 0), (0, 2), (1, 1), (3, 3), (1, 3), (3, 1), (1, 0), (0, 1), (3, 0), (0, 3))
PEERS = tuple((dx, dy, dc) for dc in (0, 1) for dx, dy in FAR) + ((0, 0, 1),)
EARLY = 12


def rem(a, n):
    return lax.rem(a, jnp.int32(n))


def hot(shape, rule):
    rows = lax.broadcasted_iota(I32, shape, 0)
    lanes = lax.broadcasted_iota(I32, shape, 1)
    return jnp.where(rule(rows, lanes), 1.0, 0.0).astype(BF16)


def dot(a, b):
    return jnp.dot(a, b, preferred_element_type=F32)


def dot_nt(a, b):
    return lax.dot_general(a, b, (((1,), (1,)), ((), ())), preferred_element_type=F32)


def kernel(table, w_hbm, m_hbm, d_ref, out_ref,
           weights, field, packed, packets, blocks, spread, pick, unpack, results, finals, give_r, give_l, take_r, take_l, sums,
           own_sem, d_send, d_recv, m_send, m_recv, w_send, w_recv, b_send, b_recv, r_send, r_recv, l_send, l_recv, f_send, f_recv):
    o, i = lax.axis_index("out"), lax.axis_index("in")
    x, y_hi, core = o // 4, rem(o // 2, 2), rem(o, 2)
    z, y_lo = i // 2, rem(i, 2)
    y = y_hi * 2 + y_lo
    me = o * 2 + y_lo

    def place(dx, dy, dc=0, dz=0):
        px, py, pc, pz = rem(x + dx, NP), rem(y + dy, NP), rem(core + dc, 2), rem(z + dz, NZ)
        return px * 4 + (py // 2) * 2 + pc, pz * 2 + rem(py, 2)

    def piece_of(device):
        return device[0] * 2 + rem(device[1], 2)

    def remote(src, dst, send, recv, device):
        return pltpu.make_async_remote_copy(src, dst, send, recv, device_id=device, device_id_type=MESH)

    up, down = place(0, 0, 0, 1), place(0, 0, 0, NZ - 1)
    up_two, down_two = place(0, 0, 0, 2), place(0, 0, 0, NZ - 2)
    devices = [place(*p) for p in PEERS]
    sources = [place(NP - p[0], NP - p[1], p[2]) for p in PEERS]
    sends = []

    def packing(rows, lanes):
        return (rows // 128 == rem(lanes, 128) // 32) & (rem(rows, 128) == (lanes // 128) * 32 + rem(lanes, 32))

    wide = hot((512, 512), packing)
    flat = d_ref[...].reshape(TERMS * OWN, ROWS)
    stacked = jnp.concatenate(
        [jnp.concatenate([flat[b * 16:(b + 1) * 16, t * 128:(t + 1) * 128] for b in range(4)], axis=1) for t in range(8)], axis=0)
    packed[...] = dot(stacked, wide).astype(BF16).reshape(8, 16, 512)

    barrier = pltpu.get_barrier_semaphore()
    for device in devices + [up, down, up_two, down_two]:
        pl.semaphore_signal(barrier, inc=1, device_id=device, device_id_type=MESH)
    pl.semaphore_wait(barrier, len(devices) + 4)

    def packet(piece):
        return packed.at[piece // 4, :, pl.ds(pl.multiple_of(rem(piece, 4) * 128, 128), 128)]

    def packet_slot(device):
        return packets.at[rem(device[1], 2), :, pl.ds(pl.multiple_of(device[0] * 128, 128), 128)]

    def run(copy):
        copy.start()
        sends.append(copy)

    for n, device in enumerate(devices):
        run(remote(packet(piece_of(device)), packet_slot((o, i)), d_send.at[n], d_recv.at[n], device))
    own_packet = pltpu.make_async_copy(packet(me), packet_slot((o, i)), own_sem.at[0])
    own_packet.start()

    def along(a, b):
        return a * (1 - core) + b * core, b * (1 - core) + a * core

    def shard(dx, dy, dc=0):
        device = place(dx, dy, dc)
        return field.at[rem(device[1], 2), pl.ds(pl.multiple_of(device[0] * FIELD, FIELD), FIELD), :]

    partner = place(0, 0, 1)
    own_field = pltpu.make_async_copy(m_hbm, shard(0, 0), own_sem.at[1])
    own_field.start()
    for n, a in enumerate(OFFSETS):
        run(remote(m_hbm, shard(0, 0), m_send.at[n], m_recv.at[n], place(*along(a, 0))))
    for n, a in enumerate(OFFSETS):
        run(remote(m_hbm, shard(0, 0), m_send.at[3 + n], m_recv.at[3 + n], place(*along(0, a))))
    run(remote(m_hbm, shard(0, 0), m_send.at[15], m_recv.at[15], partner))

    def slab(half, device):
        return weights.at[half, rem(device[1], 2), :, pl.ds(pl.multiple_of(device[0] * HALF, HALF), HALF), :]

    def rows_for(half, piece):
        return w_hbm.at[:, pl.ds(pl.multiple_of(piece * PIECE + half * HALF, HALF), HALF), :]

    def send_weights(half, first, last):
        for n in range(first, last):
            run(remote(rows_for(half, piece_of(devices[n])), slab(half, (o, i)), w_send.at[half, n], w_recv.at[half, n], devices[n]))

    for half in range(2):
        pltpu.make_async_copy(rows_for(half, me), slab(half, (o, i)), own_sem.at[2 + half]).start()
    send_weights(0, 0, EARLY)

    def unpacking(rows, lanes):
        return (rem(lanes, 128) // 16 == rows // 128) & (rem(rows, 128) == (lanes // 128) * 16 + rem(lanes, 16))

    spread[...] = hot((1024, 1024), unpacking)

    own_packet.wait()
    for n, source in enumerate(sources):
        remote(packet(me), packet_slot(source), d_send.at[n], d_recv.at[n], source).wait_recv()
    for q in range(2):
        opened = dot(packets[...].reshape(32, 2048)[:, q * 1024:(q + 1) * 1024], spread[...]).astype(BF16)
        for b in range(4):
            for half in range(2):
                for s in range(2):
                    row = (b // 2) * 64 + s * 32 + (b % 2) * 16
                    lane = (b * 2 + half) * 128
                    blocks[z, half, row:row + 16, q * 128:(q + 1) * 128] = opened[s * 16:(s + 1) * 16, lane:lane + 128]

    def ring_send(k):
        for sub in range(4):
            lot = pl.ds(sub % 2 * 64, 64)
            if k < 8:
                at = blocks.at[rem(z - k + NZ, NZ), sub // 2, lot]
                run(remote(at, at, b_send.at[0, sub, k], b_recv.at[0, sub, k], up))
            if k < 7:
                at = blocks.at[rem(z + k, NZ), sub // 2, lot]
                run(remote(at, at, b_send.at[1, sub, k], b_recv.at[1, sub, k], down))

    def ring_pass(k):
        for sub in range(4):
            lot = pl.ds(sub % 2 * 64, 64)
            at = blocks.at[rem(z - k - 1 + NZ, NZ), sub // 2, lot]
            remote(at, at, b_send.at[0, sub, k], b_recv.at[0, sub, k], down).wait_recv()
            if k < 7:
                run(remote(at, at, b_send.at[0, sub, k + 1], b_recv.at[0, sub, k + 1], up))
                at = blocks.at[rem(z + k + 1, NZ), sub // 2, lot]
                remote(at, at, b_send.at[1, sub, k], b_recv.at[1, sub, k], up).wait_recv()
                if k < 6:
                    run(remote(at, at, b_send.at[1, sub, k + 1], b_recv.at[1, sub, k + 1], down))

    ring_send(0)

    own_field.wait()
    for m, a in enumerate(OFFSETS):
        here = shard(*along(NP - a, 0))
        remote(here, here, m_send.at[m], m_recv.at[m], place(*along(a, 0))).wait_recv()
        for n, b in enumerate(OFFSETS):
            slot = 6 + m * 3 + n
            run(remote(here, here, m_send.at[slot], m_recv.at[slot], place(*along(0, b))))
        run(remote(here, here, m_send.at[16 + m], m_recv.at[16 + m], partner))

    send_weights(0, EARLY, len(PEERS))
    send_weights(1, 0, len(PEERS))

    def forward_field(m, n):
        a = 0 if m == 0 else NP - OFFSETS[m - 1]
        slot = 3 + m * 3 + n
        here = shard(*along(a, NP - OFFSETS[n]))
        remote(here, here, m_send.at[slot], m_recv.at[slot], place(*along(0, OFFSETS[n]))).wait_recv()
        back = 19 + m * 3 + n
        run(remote(here, here, m_send.at[back], m_recv.at[back], partner))

    ring_pass(0)
    ring_pass(1)

    for s in range(2):
        lanes = lax.broadcasted_iota(I32, (1, LANES), 1)
        wanted = jnp.zeros((1, LANES), I32)
        for r in range(NR):
            wanted = jnp.where(lanes // HALF == r, table[r, z * 2 + s], wanted)
        pick[s] = hot((LANES, LANES), lambda rows, cols: (rows // HALF == wanted) & (rem(rows, HALF) == rem(cols, HALF)))

    def closing(rows, lanes):
        inner = rem(lanes, 128)
        return (inner // 16 == rows // 128) & (rem(rows, 128) == (lanes // 128) * 16 + rem(lanes, 16))

    spread[0:512, :] = hot((512, 1024), closing)
    for b in range(2):
        unpack[b] = hot((512, 128), lambda rows, lanes: (rows // 128 == lanes // 32) & (rem(rows, 128) == b * 32 + rem(lanes, 32)))

    ring_pass(2)
    ring_pass(3)
    for n in range(3):
        forward_field(0, n)
    ring_pass(4)
    for m in range(1, 4):
        for n in range(3):
            forward_field(m, n)
    for k in range(5, 8):
        ring_pass(k)

    for n in range(16):
        if n == 0:
            here = shard(0, 0, 1)
        elif n < 4:
            a = NP - OFFSETS[n - 1]
            here = shard(a * core, a * (1 - core), 1)
        else:
            m, q = (n - 4) // 3, (n - 4) % 3
            a = 0 if m == 0 else NP - OFFSETS[m - 1]
            b = NP - OFFSETS[q]
            here = shard(a * core + b * (1 - core), b * core + a * (1 - core), 1)
        remote(here, here, m_send.at[15 + n], m_recv.at[15 + n], partner).wait_recv()

    def chunk_terms(half, chunks):
        n = len(chunks)
        totals = [None] * n
        for s in range(2):
            cells = jnp.concatenate([field[s, pl.ds(pl.multiple_of(c * CHUNK, CHUNK), CHUNK), :] for c in chunks], axis=0)
            product = dot_nt(cells, weights[half, s].reshape(TERMS * LANES, DEPTH))
            chosen = dot(jnp.concatenate([blocks[c, half] for c in chunks], axis=0), pick[s])
            for m in range(n):
                for t in range(TERMS):
                    scale = chosen[(m * TERMS + t) * CHUNK:(m * TERMS + t + 1) * CHUNK]
                    part = scale * product[m * CHUNK:(m + 1) * CHUNK, t * LANES:(t + 1) * LANES]
                    totals[m] = part if totals[m] is None else totals[m] + part
        return totals

    def right(half, k, sub):
        target = up_two if k in (1, 3, 5) else up
        return remote(give_r.at[half, k, sub], take_r.at[half, k, sub], r_send.at[half, k, sub], r_recv.at[half, k, sub], target)

    def left(half, k, sub):
        target = down_two if k in (0, 2, 4) else down
        return remote(give_l.at[half, k, sub], take_l.at[half, k, sub], l_send.at[half, k, sub], l_recv.at[half, k, sub], target)

    def pass_on(half, k, move, give, take):
        for sub in range(2):
            move(half, k - 1, sub).wait_recv()
            value = give[half, k, sub] + take[half, k - 1, sub]
            if k >= 2 + k % 2:
                move(half, k - 2, sub).wait_recv()
                value = value + take[half, k - 2, sub]
            give[half, k, sub] = value
            move(half, k, sub).start()

    def reduce_half(half, carry):
        pltpu.make_async_copy(rows_for(half, me), slab(half, (o, i)), own_sem.at[2 + half]).wait()
        for n, source in enumerate(sources):
            remote(rows_for(half, me), slab(half, source), w_send.at[half, n], w_recv.at[half, n], source).wait_recv()
        for step in range(0, 8, 2):
            terms = chunk_terms(half, [rem(z + 8 - step, NZ), rem(z + 7 - step + NZ, NZ), rem(z + 9 + step, NZ), rem(z + 10 + step, NZ)])
            for sub in range(2):
                for k in range(2):
                    give_r[half, step + k, sub] = terms[k][:, sub * 128:(sub + 1) * 128]
                    give_l[half, step + k, sub] = terms[2 + k][:, sub * 128:(sub + 1) * 128]
                right(half, step, sub).start()
                if step < 6:
                    left(half, step + 1, sub).start()
                if step == 0:
                    left(half, 0, sub).start()
            if step == 0:
                @pl.when(half == 1)
                def _():
                    pass_on(0, 7, right, give_r, take_r)
            if step > 0:
                pass_on(half, step - 1, right, give_r, take_r)
                pass_on(half, step, left, give_l, take_l)
        return carry

    lax.fori_loop(0, 2, reduce_half, jnp.int32(0))
    pass_on(1, 7, right, give_r, take_r)

    for half in range(2):
        for sub in range(2):
            left(half, 6, sub).wait_recv()
            right(half, 7, sub).wait_recv()
            total = give_l[half, 7, sub] + take_l[half, 6, sub] + take_r[half, 7, sub]
            sums[half * 2 + sub] = total.astype(BF16)

    closed = jnp.concatenate(
        [jnp.concatenate([sums[half * 2 + q, s * 32 + b * 16:s * 32 + b * 16 + 16, :] for b in range(2) for half in range(2)], axis=1)
         for s in range(2) for q in range(2)], axis=0)
    results[...] = dot(closed, spread[0:512, :]).astype(BF16).reshape(2, 2, 16, 1024)

    def result_for(device):
        return results.at[rem(device[1], 2), device[0] // 8, :, pl.ds(pl.multiple_of(rem(device[0], 8) * 128, 128), 128)]

    def result_slot(piece):
        return finals.at[piece // 4, :, pl.ds(pl.multiple_of(rem(piece, 4) * 128, 128), 128)]

    for n, device in enumerate(devices):
        run(remote(result_for(device), result_slot(me), f_send.at[n], f_recv.at[n], device))
    own_result = pltpu.make_async_copy(result_for((o, i)), result_slot(me), own_sem.at[4])
    own_result.start()

    for copy in sends[:-len(devices)]:
        copy.wait_send()
    for half in range(2):
        for sub in range(2):
            for k in range(8):
                right(half, k, sub).wait_send()
                if k < 7:
                    left(half, k, sub).wait_send()

    own_result.wait()
    for n, source in enumerate(sources):
        remote(result_for(source), result_slot(piece_of(source)), f_send.at[n], f_recv.at[n], source).wait_recv()
    for b in range(2):
        opened = dot(finals[...].reshape(128, 512), unpack[b]).astype(BF16)
        for j in range(8):
            out_ref[b * 16:(b + 1) * 16, j * 128:(j + 1) * 128] = opened[j * 16:(j + 1) * 16, :]
    for copy in sends[-len(devices):]:
        copy.wait_send()


def shards(kernel_weights, mode_field, diff_blocks, block_table):
    peers = len(PEERS)
    dma = pltpu.SemaphoreType.DMA
    vmem = pl.BlockSpec(memory_space=pltpu.VMEM)
    gain = pl.pallas_call(
        kernel,
        out_shape=jax.ShapeDtypeStruct((OWN, ROWS), BF16),
        in_specs=[pl.BlockSpec(memory_space=pltpu.SMEM), pl.BlockSpec(memory_space=pl.ANY),
                  pl.BlockSpec(memory_space=pl.ANY), vmem],
        out_specs=vmem,
        scratch_shapes=[
            pltpu.VMEM((2, 2, TERMS, LANES, DEPTH), BF16),
            pltpu.VMEM((2, CELLS, DEPTH), BF16),
            pltpu.VMEM((8, 16, 512), BF16),
            pltpu.VMEM((2, 16, 2048), BF16),
            pltpu.VMEM((NZ, 2, TERMS * CHUNK, LANES), BF16),
            pltpu.VMEM((1024, 1024), BF16),
            pltpu.VMEM((2, LANES, LANES), BF16),
            pltpu.VMEM((2, 512, 128), BF16),
            pltpu.VMEM((2, 2, 16, 1024), BF16),
            pltpu.VMEM((8, 16, 512), BF16),
            pltpu.VMEM((2, 8, 2, CHUNK, 128), F32),
            pltpu.VMEM((2, 8, 2, CHUNK, 128), F32),
            pltpu.VMEM((2, 8, 2, CHUNK, 128), F32),
            pltpu.VMEM((2, 8, 2, CHUNK, 128), F32),
            pltpu.VMEM((4, CHUNK, 128), BF16),
            dma((5,)),
            dma((peers,)), dma((peers,)),
            dma((31,)), dma((31,)),
            dma((2, peers)), dma((2, peers)),
            dma((2, 4, 8)), dma((2, 4, 8)),
            dma((2, 8, 2)), dma((2, 8, 2)),
            dma((2, 8, 2)), dma((2, 8, 2)),
            dma((peers,)), dma((peers,)),
        ],
        compiler_params=pltpu.CompilerParams(collective_id=0, has_side_effects=True, vmem_limit_bytes=63 * 2**20),
        name="collision_gain",
    )(block_table, kernel_weights, mode_field.T, diff_blocks.transpose(0, 2, 1))
    return gain.T


def solution(mesh):
    in_specs = (P(None, "out", "in"), P("in", "out"), P(None, "out", "in"), P())
    return jax.shard_map(shards, mesh=mesh, in_specs=in_specs, out_specs=P("out", "in"), check_vma=False)
```
